32 devices in a mesh: fsdp: 8 (over y, x, core), group: 4 (over z).
Axes of the slice: x: 2, y: 2, z: 4, core: 2. Of those that a mesh axis runs over, the one named last changes fastest.
Arguments:
- gradient: bfloat16 [4, 512, 4096], P('group', 'fsdp'), may hold values from -4000 to 4000
- first_moment: bfloat16 [4, 4096, 512], P('group', 'fsdp'), may hold values from -3 to 3
- second_moment: bfloat16 [4, 4096, 512], P('group', 'fsdp'), may hold values from 0.29882812 to 3
- basis_store: bfloat16 [4, 4608, 256], P('group', 'fsdp'), may hold values from -1 to 2
- step_number: int32 [1], replicated, may hold values from 1 to 99999
- matrix_ids: int32 [4], P('group'), may hold values from 0 to 3, each once
Outputs:
- update: bfloat16 [4, 512, 4096], P('group', 'fsdp')
- new_first: bfloat16 [4, 4096, 512], P('group', 'fsdp')
- new_second: bfloat16 [4, 4096, 512], P('group', 'fsdp')
The draws below stay inside these ranges and needn't reach their ends.
Inputs may be any that keep to these rules, and one draw needn't show every extreme that they name: `matrix_ids`: each matrix index once.
All inputs are finite; a program needn't handle non-finite values.
Results may differ from the reference program's by a relative error of at most 0.0004.
Values may be sent and summed in bfloat16 or wider, within the bound.
A program may use at most 64 MiB of HBM per device.

```python
import math
import jax
import jax.numpy as jnp
from jax import lax

COLS = 4096
BLOCK = 256
ROWS = 512
MATS = 4
BROWS = 4608
OWNER_ROWS = 576
LEFT_BLOCKS = 2
RIGHT_BLOCKS = 16
ELEMS = 8388608
N_FSDP = 8


def draw_gradient(key, part):
    key_base, key_cols = jax.random.split(key, 2)
    place = jnp.arange(ROWS, dtype=jnp.float32) / ROWS
    col_scale = jnp.exp(jax.random.uniform(key_cols, (COLS,), jnp.float32, 0.0, math.log(10.0)))
    mat_scale = 1.0 + 2.0 * jnp.arange(MATS, dtype=jnp.float32) / max(MATS - 1, 1)
    base = jax.random.truncated_normal(key_base, -6.0, 6.0, (MATS, ROWS, COLS), jnp.float32)
    row_scale = jnp.power(10.0, place)
    values = 2.0 * base * mat_scale[:, None, None] * row_scale[None, :, None] * col_scale[None, None, :]
    return values.astype(jnp.bfloat16)


def draw_basis_store(key, part):
    noise = jax.random.truncated_normal(key, -6.0, 6.0, (MATS, BROWS, BLOCK), jnp.float32)
    noise = noise * (0.25 / math.sqrt(BLOCK))
    unit = (jnp.arange(BROWS)[:, None] % BLOCK == jnp.arange(BLOCK)[None, :]).astype(jnp.float32)
    return (unit[None, :, :] + noise).astype(jnp.bfloat16)


def steps_of(stream_key, shape, pieces, least, largest):
    loudness = 1.0
    for position, parts in pieces:
        heights = jax.random.uniform(jax.random.fold_in(jax.random.fold_in(stream_key, 6), position), (parts,), jnp.float32, least / len(pieces), largest / len(pieces))
        loudness = loudness * jnp.repeat(jnp.exp(heights), shape[position] // parts).reshape((-1,) + (1,) * (len(shape) - 1 - position))
    return loudness


def gaussian(key, extent, deviation, limit, cuts=(), kind=jnp.bfloat16):
    entries = deviation * jax.random.normal(key, extent, jnp.float32)
    if cuts:
        entries = entries * steps_of(key, extent, cuts, -0.22, 0.18)
    return jnp.clip(entries, -limit, limit).astype(kind)


def setup_inputs(seed: int = 0) -> dict:
    streams_of = jax.random.split(jax.random.key(seed), 7)
    gradient = draw_gradient(jax.random.fold_in(streams_of[6], 71), 0)
    first_moment = gaussian(streams_of[1], (MATS, COLS, ROWS), 0.5, 3.0, ((0, 4), (1, 8)))
    second_moment = jnp.clip(jnp.exp(math.log(3.0) - 2.306499 * jax.random.uniform(streams_of[2], (MATS, COLS, ROWS), jnp.float32) ** steps_of(streams_of[2], (MATS, COLS, ROWS), ((0, 4), (1, 8)), -0.2, 0.2)), 0.29882812, 3.0).astype(jnp.bfloat16)
    basis_store = draw_basis_store(jax.random.fold_in(streams_of[6], 71), 0)
    step_number = jax.random.randint(streams_of[4], (1,), 1, 100000).astype(jnp.int32)
    matrix_ids = jax.random.permutation(streams_of[5], MATS).astype(jnp.int32)
    return {"gradient": gradient, "first_moment": first_moment, "second_moment": second_moment, "basis_store": basis_store, "step_number": step_number, "matrix_ids": matrix_ids}


BETA_ONE = 0.95
BETA_TWO = 0.95
ADAM_EPS = 1e-08
HIGHEST = lax.Precision.HIGHEST

def reference(gradient, first_moment, second_moment, basis_store, step_number, matrix_ids):
    total = jnp.float32(0.0)
    for index in range(MATS):
        single = gradient[index].astype(jnp.float32)
        total = total + jnp.sum(single * single)
    clip = jnp.sqrt(jnp.float32(ELEMS)) / (jnp.sqrt(total) + 1e-06)
    count = step_number[0].astype(jnp.float32)
    first_fix = 1.0 - jnp.power(jnp.float32(BETA_ONE), count)
    second_fix = 1.0 - jnp.power(jnp.float32(BETA_TWO), count)
    updates = []
    firsts = []
    seconds = []
    for index in range(MATS):
        shift = ((step_number[0] + matrix_ids[index]) % N_FSDP).astype(jnp.int32) * OWNER_ROWS
        ordered = jnp.roll(basis_store[index], -shift, axis=0).astype(jnp.float32)
        left = ordered[:ROWS].reshape(LEFT_BLOCKS, BLOCK, BLOCK)
        right = ordered[ROWS:].reshape(RIGHT_BLOCKS, BLOCK, BLOCK)
        plain = gradient[index].astype(jnp.float32)
        turned = jnp.einsum('rbj,bjl->rbl', plain.reshape(ROWS, RIGHT_BLOCKS, BLOCK), right, precision=HIGHEST).reshape(ROWS, COLS)
        turned = clip * turned
        rotated = jnp.einsum('bkc,bki->cbi', turned.reshape(LEFT_BLOCKS, BLOCK, COLS), left, precision=HIGHEST).reshape(COLS, ROWS)
        first_sum = BETA_ONE * first_moment[index].astype(jnp.float32) + (1.0 - BETA_ONE) * rotated
        second_sum = BETA_TWO * second_moment[index].astype(jnp.float32) + (1.0 - BETA_TWO) * rotated * rotated
        direction = first_sum / first_fix / (jnp.sqrt(second_sum / second_fix) + ADAM_EPS)
        backward = jnp.einsum('cbi,bki->cbk', direction.reshape(COLS, LEFT_BLOCKS, BLOCK), left, precision=HIGHEST).reshape(COLS, ROWS)
        result = jnp.einsum('blr,bjl->rbj', backward.reshape(RIGHT_BLOCKS, BLOCK, ROWS), right, precision=HIGHEST).reshape(ROWS, COLS)
        updates.append(result.astype(jnp.bfloat16))
        firsts.append(first_sum.astype(jnp.bfloat16))
        seconds.append(second_sum.astype(jnp.bfloat16))
    return (jnp.stack(updates), jnp.stack(firsts), jnp.stack(seconds))
```

```python
import functools
import math

import jax
import jax.numpy as jnp
from jax import lax
from jax.experimental import pallas as pl
from jax.experimental.pallas import tpu as pltpu
from jax.sharding import PartitionSpec as P

BLOCK = 256


BETA_ONE = 0.95
BETA_TWO = 0.95
ADAM_EPS = 1e-08
HIGHEST = lax.Precision.HIGHEST


def clip_of(local_squares, entries):
    total = lax.psum(local_squares, ("fsdp", "group"))
    return jnp.float32(math.sqrt(entries)) / (jnp.sqrt(total) + 1e-06)


def local_general(gradient, first_moment, second_moment, basis_store, step_number, matrix_ids):
    fsdp_count = lax.axis_size("fsdp")
    group_count = lax.axis_size("group")
    row_count = gradient.shape[1]
    col_count = gradient.shape[2]
    all_rows = row_count * fsdp_count
    col_share = col_count // fsdp_count
    left_blocks = all_rows // BLOCK
    right_blocks = col_count // BLOCK
    entries = all_rows * col_count * group_count
    grad_local = gradient[0].astype(jnp.float32)
    local_squares = jnp.sum(grad_local * grad_local)
    gathered = lax.all_gather(basis_store[0], "fsdp", axis=0, tiled=True)
    owner_rows = basis_store.shape[1]
    owner = (step_number[0] + matrix_ids[0]) % fsdp_count
    ordered_half = jnp.roll(gathered, -owner * owner_rows, axis=0)
    left = ordered_half[:all_rows].astype(jnp.float32).reshape(left_blocks, BLOCK, BLOCK)
    right_half = ordered_half[all_rows:].reshape(right_blocks, BLOCK, BLOCK)
    right = right_half.astype(jnp.float32)
    turned = jnp.einsum(
        "rbj,bjl->rbl",
        gradient[0].reshape(row_count, right_blocks, BLOCK),
        right_half,
        preferred_element_type=jnp.float32,
    )
    turned = clip_of(local_squares, entries) * turned
    outgoing = turned.reshape(row_count, fsdp_count, col_share)
    received = lax.all_to_all(outgoing, "fsdp", split_axis=1, concat_axis=0, tiled=True)
    width = received.shape[2]
    columns = received[:, 0, :].reshape(left_blocks, BLOCK, width)
    rotated = jnp.einsum("bkc,bki->cbi", columns, left, precision=HIGHEST).reshape(width, all_rows)
    count = step_number[0].astype(jnp.float32)
    first_fix = 1.0 - jnp.power(jnp.float32(BETA_ONE), count)
    second_fix = 1.0 - jnp.power(jnp.float32(BETA_TWO), count)
    first_sum = BETA_ONE * first_moment[0].astype(jnp.float32) + (1.0 - BETA_ONE) * rotated
    second_sum = (
        BETA_TWO * second_moment[0].astype(jnp.float32) + (1.0 - BETA_TWO) * rotated * rotated
    )
    direction = first_sum / first_fix / (jnp.sqrt(second_sum / second_fix) + ADAM_EPS)
    backward = jnp.einsum(
        "cbi,bki->cbk", direction.reshape(col_share, left_blocks, BLOCK), left, precision=HIGHEST
    )
    returning = backward.reshape(col_share, fsdp_count, row_count)
    received = lax.all_to_all(returning, "fsdp", split_axis=1, concat_axis=0, tiled=True)
    width = received.shape[2]
    pieces = received[:, 0, :].reshape(right_blocks, BLOCK, width)
    result = jnp.einsum("blr,bjl->rbj", pieces, right, precision=HIGHEST).reshape(width, col_count)
    return (
        result[None].astype(jnp.bfloat16),
        first_sum[None].astype(jnp.bfloat16),
        second_sum[None].astype(jnp.bfloat16),
    )


SLAB = 16
LANES = 128
MESH = pl.DeviceIdType.MESH


def pieces_of(x):
    high = x.astype(jnp.bfloat16)
    rest = x - high.astype(jnp.float32)
    middle = rest.astype(jnp.bfloat16)
    low = (rest - middle.astype(jnp.float32)).astype(jnp.bfloat16)
    return high, middle, low


def mm(a, b, dims):
    return lax.dot_general(a, b, (dims, ((), ())), preferred_element_type=jnp.float32)


NN = ((1,), (0,))
NT = ((1,), (1,))


def kernel(n, groups, grad, first, second, basis, step, ident, out_u, out_1, out_2,
           own, m1, m2, hop, staged, left, right, got, n1, n2, upd, sq_own, sq_z, sq_mid, sq_f,
           loc, hop_s, hop_r, left_s, left_r, right_s, right_r, got_s, got_r,
           ret_s, ret_r, z_s, z_r, f_s, f_r):
    me = lax.axis_index("fsdp")
    zz = lax.axis_index("group")
    share = grad.shape[1]
    cols = grad.shape[2]
    width = cols // n
    halves = width // BLOCK
    slabs = n // 2
    per_owner = basis.shape[0]
    span = slabs * SLAB
    left_groups = left.shape[0]
    block_groups = BLOCK // span
    entries = float(share * n * cols * groups)

    def peer(k):
        return lax.rem(me + k, n)

    def zpeer(k):
        return lax.rem(zz + k, groups)

    def lanes_of(c):
        return pl.ds(pl.multiple_of(lax.rem(c, 2) * LANES, LANES), LANES)

    def rows_of(c):
        return pl.ds(pl.multiple_of((c // 2) * SLAB, SLAB), SLAB)

    def share_rows(d):
        return pl.ds(pl.multiple_of(d * share, share), share)

    def out_cols(d, t):
        return pl.ds(pl.multiple_of(d * width + t * BLOCK, BLOCK), BLOCK)

    def remote(src, dst, ssem, rsem, k):
        return pltpu.make_async_remote_copy(
            src_ref=src, dst_ref=dst, send_sem=ssem, recv_sem=rsem,
            device_id={"fsdp": peer(k)}, device_id_type=MESH)

    locals_ = [
        pltpu.make_async_copy(grad.at[0], own, loc.at[0]),
        pltpu.make_async_copy(basis.at[:, me // 2, :, lanes_of(me)], hop.at[me], loc.at[1]),
        pltpu.make_async_copy(first.at[0], m1, loc.at[2]),
        pltpu.make_async_copy(second.at[0], m2, loc.at[3]),
    ]
    for t in range(halves):
        locals_.append(pltpu.make_async_copy(
            grad.at[0, :, out_cols(me, t)], got.at[t, share_rows(me)], loc.at[4 + t]))
    for copy in locals_:
        copy.start()

    barrier = pltpu.get_barrier_semaphore()
    for k in range(1, n):
        pl.semaphore_signal(barrier, inc=1, device_id={"fsdp": peer(k)}, device_id_type=MESH)
    for k in range(1, groups):
        pl.semaphore_signal(barrier, inc=1, device_id={"group": zpeer(k)}, device_id_type=MESH)
    pl.semaphore_wait(barrier, n - 1 + groups - 1)

    hops = []
    for k in range(1, n):
        c = peer(k)
        hops.append(remote(basis.at[:, c // 2, :, lanes_of(c)], hop.at[me],
                           hop_s.at[k], hop_r.at[k], k))
        hops[-1].start()

    gots = [[None] * n for _ in range(halves)]

    def send_got(t):
        for k in range(1, n):
            gots[t][k] = remote(grad.at[0, :, out_cols(peer(k), t)], got.at[t, share_rows(me)],
                                got_s.at[t, k], got_r.at[t, k], k)
            gots[t][k].start()

    send_got(0)

    locals_[0].wait()
    squares = jnp.zeros((8, LANES), jnp.float32)
    for r in range(0, share, 16):
        rows = own[r:r + 16, :].astype(jnp.float32)
        rows = rows * rows
        rows = rows[0:8] + rows[8:16]
        for c in range(0, cols, LANES):
            squares = squares + rows[:, c:c + LANES]
    sq_own[...] = squares
    zs = []
    for k in range(1, groups):
        zs.append(pltpu.make_async_remote_copy(
            src_ref=sq_own, dst_ref=sq_z.at[k], send_sem=z_s.at[k], recv_sem=z_r.at[k],
            device_id={"group": zpeer(k)}, device_id_type=MESH))
        zs[-1].start()

    for copy in hops:
        copy.wait_recv()
    locals_[1].wait()
    owner = lax.rem(step[0] + ident[0], n)
    for q in range(n):
        staged[q * per_owner:(q + 1) * per_owner] = hop[lax.rem(owner + q, n)]

    rights = [[None] * n for _ in range(halves)]

    def send_right(t):
        for k in range(n):
            d = peer(k)
            src = staged.at[pl.ds(left_groups + (d * halves + t) * block_groups, block_groups)]
            dst = right.at[t, :, rows_of(me), lanes_of(me)]
            if k == 0:
                rights[t][k] = pltpu.make_async_copy(src, dst, right_r.at[t, 0])
            else:
                rights[t][k] = remote(src, dst, right_s.at[t, k], right_r.at[t, k], k)
            rights[t][k].start()

    send_right(0)
    lefts = []
    for k in range(n):
        src = staged.at[pl.ds(0, left_groups)]
        dst = left.at[:, rows_of(me), lanes_of(me)]
        if k == 0:
            lefts.append(pltpu.make_async_copy(src, dst, left_r.at[0]))
        else:
            lefts.append(remote(src, dst, left_s.at[k], left_r.at[k], k))
        lefts[-1].start()
    for t in range(1, halves):
        send_got(t)
        send_right(t)

    squares = sq_own[...]
    for k, copy in enumerate(zs):
        copy.wait_recv()
        squares = squares + sq_z[k + 1]
    sq_mid[...] = squares
    fs = []
    for k in range(1, n):
        fs.append(remote(sq_mid, sq_f.at[k], f_s.at[k], f_r.at[k], k))
        fs[-1].start()
    for k, copy in enumerate(fs):
        copy.wait_recv()
        squares = squares + sq_f[k + 1]
    total = jnp.sum(squares, keepdims=True)
    clip = jnp.float32(math.sqrt(entries)) / (jnp.sqrt(total) + 1e-06)
    count = jnp.full((1, 1), step[0].astype(jnp.float32))
    first_inv = 1.0 / (1.0 - jnp.exp(count * jnp.float32(math.log(BETA_ONE))))
    second_inv = 1.0 / (1.0 - jnp.exp(count * jnp.float32(math.log(BETA_TWO))))

    locals_[2].wait()
    locals_[3].wait()
    all_rows = share * n
    left_blocks = all_rows // BLOCK
    returns = []
    outs = []
    for t in range(halves):
        for copy in rights[t][1:]:
            copy.wait_recv()
        rights[t][0].wait()
        if t == 0:
            for copy in lefts[1:]:
                copy.wait_recv()
            lefts[0].wait()
        for k in range(1, n):
            gots[t][k].wait_recv()
        locals_[4 + t].wait()
        rt = right[t].reshape(BLOCK, BLOCK)
        flipped = rt.astype(jnp.float32).T.astype(jnp.bfloat16)
        cut = slice(t * BLOCK, (t + 1) * BLOCK)
        for b in range(left_blocks):
            cols_b = slice(b * BLOCK, (b + 1) * BLOCK)
            lb = left[b * block_groups:(b + 1) * block_groups].reshape(BLOCK, BLOCK)
            turned = mm(flipped, got[t, cols_b, :], NT)
            rotated = sum(mm(piece, lb, NN) for piece in pieces_of(turned)) * clip
            first_sum = BETA_ONE * m1[cut, cols_b].astype(jnp.float32) + (1.0 - BETA_ONE) * rotated
            second_sum = (BETA_TWO * m2[cut, cols_b].astype(jnp.float32)
                          + (1.0 - BETA_TWO) * rotated * rotated)
            n1[cut, cols_b] = first_sum.astype(jnp.bfloat16)
            n2[cut, cols_b] = second_sum.astype(jnp.bfloat16)
            direction = first_sum * first_inv / (jnp.sqrt(second_sum * second_inv) + ADAM_EPS)
            back = sum(mm(rt, piece, NN) for piece in pieces_of(direction))
            result = sum(mm(lb, piece, NT) for piece in pieces_of(back))
            upd[t, cols_b, :] = result.astype(jnp.bfloat16)
        for k in range(n):
            src = upd.at[t, share_rows(peer(k))]
            dst = out_u.at[0, :, out_cols(me, t)]
            if k == 0:
                copy = pltpu.make_async_copy(src, dst, ret_r.at[t, 0])
                outs.append(copy)
            else:
                copy = remote(src, dst, ret_s.at[t, k], ret_r.at[t, k], k)
                returns.append(copy)
            copy.start()
        for index, (value, target) in enumerate(((n1, out_1), (n2, out_2))):
            copy = pltpu.make_async_copy(
                value.at[cut], target.at[0, cut], loc.at[4 + halves + 2 * t + index])
            copy.start()
            outs.append(copy)

    for copy in hops + zs + fs + lefts[1:]:
        copy.wait_send()
    for t in range(halves):
        for k in range(1, n):
            gots[t][k].wait_send()
            rights[t][k].wait_send()
    for copy in outs:
        copy.wait()
    for copy in returns:
        copy.wait()


def fits(gradient, first_moment, basis_store, n):
    if n % 2:
        return False
    span = n // 2 * SLAB
    width = gradient.shape[2] // n
    all_rows = gradient.shape[1] * n
    return (
        BLOCK % span == 0
        and basis_store.shape[1] % span == 0
        and width % BLOCK == 0
        and all_rows % BLOCK == 0
        and gradient.shape[1] % SLAB == 0
        and all_rows <= 1024
        and width <= 1024
    )


def local(gradient, first_moment, second_moment, basis_store, step_number, matrix_ids):
    n = lax.axis_size("fsdp")
    groups = lax.axis_size("group")
    if not fits(gradient, first_moment, basis_store, n):
        return local_general(
            gradient, first_moment, second_moment, basis_store, step_number, matrix_ids
        )
    share, cols = gradient.shape[1:]
    all_rows = share * n
    width = cols // n
    halves = width // BLOCK
    slabs = n // 2
    span = slabs * SLAB
    per_owner = basis_store.shape[1] // span
    basis = basis_store.reshape(per_owner, slabs, SLAB, BLOCK)
    half = jnp.bfloat16
    anywhere = pl.BlockSpec(memory_space=pl.ANY)
    scalar = pl.BlockSpec(memory_space=pltpu.SMEM)
    dma = pltpu.SemaphoreType.DMA
    tile = (8, LANES)
    return pl.pallas_call(
        functools.partial(kernel, n, groups),
        out_shape=(
            jax.ShapeDtypeStruct(gradient.shape, half),
            jax.ShapeDtypeStruct(first_moment.shape, half),
            jax.ShapeDtypeStruct(second_moment.shape, half),
        ),
        in_specs=[anywhere] * 4 + [scalar] * 2,
        out_specs=(anywhere,) * 3,
        scratch_shapes=[
            pltpu.VMEM((share, cols), half),
            pltpu.VMEM((width, all_rows), half),
            pltpu.VMEM((width, all_rows), half),
            pltpu.VMEM((n, per_owner, SLAB, LANES), half),
            pltpu.VMEM((n * per_owner, SLAB, LANES), half),
            pltpu.VMEM((all_rows // span, span, BLOCK), half),
            pltpu.VMEM((halves, BLOCK // span, span, BLOCK), half),
            pltpu.VMEM((halves, all_rows, BLOCK), half),
            pltpu.VMEM((width, all_rows), half),
            pltpu.VMEM((width, all_rows), half),
            pltpu.VMEM((halves, all_rows, BLOCK), half),
            pltpu.VMEM(tile, jnp.float32),
            pltpu.VMEM((groups,) + tile, jnp.float32),
            pltpu.VMEM(tile, jnp.float32),
            pltpu.VMEM((n,) + tile, jnp.float32),
            dma((4 + 3 * halves,)),
            dma((n,)), dma((n,)),
            dma((n,)), dma((n,)),
            dma((halves, n)), dma((halves, n)),
            dma((halves, n)), dma((halves, n)),
            dma((halves, n)), dma((halves, n)),
            dma((groups,)), dma((groups,)),
            dma((n,)), dma((n,)),
        ],
        compiler_params=pltpu.CompilerParams(
            collective_id=0, has_side_effects=True, vmem_limit_bytes=32 << 20
        ),
    )(gradient, first_moment, second_moment, basis, step_number, matrix_ids)


def solution(mesh):
    in_specs = (
        P("group", "fsdp", None),
        P("group", "fsdp", None),
        P("group", "fsdp", None),
        P("group", "fsdp", None),
        P(),
        P("group"),
    )
    out_specs = (P("group", "fsdp", None), P("group", "fsdp", None), P("group", "fsdp", None))
    return jax.shard_map(local, mesh=mesh, in_specs=in_specs, out_specs=out_specs, check_vma=False)
```

```python
import functools
import math

import jax
import jax.numpy as jnp
from jax import lax
from jax.experimental import pallas as pl
from jax.experimental.pallas import tpu as pltpu
from jax.sharding import PartitionSpec as P

BLOCK = 256


BETA_ONE = 0.95
BETA_TWO = 0.95
ADAM_EPS = 1e-08
HIGHEST = lax.Precision.HIGHEST


def clip_of(local_squares, entries):
    total = lax.psum(local_squares, ("fsdp", "group"))
    return jnp.float32(math.sqrt(entries)) / (jnp.sqrt(total) + 1e-06)


def local_general(gradient, first_moment, second_moment, basis_store, step_number, matrix_ids):
    fsdp_count = lax.axis_size("fsdp")
    group_count = lax.axis_size("group")
    row_count = gradient.shape[1]
    col_count = gradient.shape[2]
    all_rows = row_count * fsdp_count
    col_share = col_count // fsdp_count
    left_blocks = all_rows // BLOCK
    right_blocks = col_count // BLOCK
    entries = all_rows * col_count * group_count
    grad_local = gradient[0].astype(jnp.float32)
    local_squares = jnp.sum(grad_local * grad_local)
    gathered = lax.all_gather(basis_store[0], "fsdp", axis=0, tiled=True)
    owner_rows = basis_store.shape[1]
    owner = (step_number[0] + matrix_ids[0]) % fsdp_count
    ordered_half = jnp.roll(gathered, -owner * owner_rows, axis=0)
    left = ordered_half[:all_rows].astype(jnp.float32).reshape(left_blocks, BLOCK, BLOCK)
    right_half = ordered_half[all_rows:].reshape(right_blocks, BLOCK, BLOCK)
    right = right_half.astype(jnp.float32)
    turned = jnp.einsum(
        "rbj,bjl->rbl",
        gradient[0].reshape(row_count, right_blocks, BLOCK),
        right_half,
        preferred_element_type=jnp.float32,
    )
    turned = clip_of(local_squares, entries) * turned
    outgoing = turned.reshape(row_count, fsdp_count, col_share)
    received = lax.all_to_all(outgoing, "fsdp", split_axis=1, concat_axis=0, tiled=True)
    width = received.shape[2]
    columns = received[:, 0, :].reshape(left_blocks, BLOCK, width)
    rotated = jnp.einsum("bkc,bki->cbi", columns, left, precision=HIGHEST).reshape(width, all_rows)
    count = step_number[0].astype(jnp.float32)
    first_fix = 1.0 - jnp.power(jnp.float32(BETA_ONE), count)
    second_fix = 1.0 - jnp.power(jnp.float32(BETA_TWO), count)
    first_sum = BETA_ONE * first_moment[0].astype(jnp.float32) + (1.0 - BETA_ONE) * rotated
    second_sum = (
        BETA_TWO * second_moment[0].astype(jnp.float32) + (1.0 - BETA_TWO) * rotated * rotated
    )
    direction = first_sum / first_fix / (jnp.sqrt(second_sum / second_fix) + ADAM_EPS)
    backward = jnp.einsum(
        "cbi,bki->cbk", direction.reshape(col_share, left_blocks, BLOCK), left, precision=HIGHEST
    )
    returning = backward.reshape(col_share, fsdp_count, row_count)
    received = lax.all_to_all(returning, "fsdp", split_axis=1, concat_axis=0, tiled=True)
    width = received.shape[2]
    pieces = received[:, 0, :].reshape(right_blocks, BLOCK, width)
    result = jnp.einsum("blr,bjl->rbj", pieces, right, precision=HIGHEST).reshape(width, col_count)
    return (
        result[None].astype(jnp.bfloat16),
        first_sum[None].astype(jnp.bfloat16),
        second_sum[None].astype(jnp.bfloat16),
    )


SLAB = 16
LANES = 128
MESH = pl.DeviceIdType.MESH


def pieces_of(x):
    high = x.astype(jnp.bfloat16)
    rest = x - high.astype(jnp.float32)
    middle = rest.astype(jnp.bfloat16)
    low = (rest - middle.astype(jnp.float32)).astype(jnp.bfloat16)
    return high, middle, low


def mm(a, b, dims):
    return lax.dot_general(a, b, (dims, ((), ())), preferred_element_type=jnp.float32)


NN = ((1,), (0,))
NT = ((1,), (1,))


def kernel(n, groups, grad, first, second, basis, step, ident, out_u, out_1, out_2,
           own, m1, m2, hop, staged, left, right, got, n1, n2, upd, sq_own, sq_z, sq_mid, sq_f,
           loc, hop_s, hop_r, left_s, left_r, right_s, right_r, got_s, got_r,
           ret_s, ret_r, z_s, z_r, f_s, f_r):
    me = lax.axis_index("fsdp")
    zz = lax.axis_index("group")
    share = grad.shape[1]
    cols = grad.shape[2]
    width = cols // n
    halves = width // BLOCK
    slabs = n // 2
    per_owner = basis.shape[0]
    span = slabs * SLAB
    left_groups = left.shape[0]
    block_groups = BLOCK // span
    entries = float(share * n * cols * groups)

    def peer(k):
        return lax.rem(me + k, n)

    def zpeer(k):
        return lax.rem(zz + k, groups)

    def lanes_of(c):
        return pl.ds(pl.multiple_of(lax.rem(c, 2) * LANES, LANES), LANES)

    def rows_of(c):
        return pl.ds(pl.multiple_of((c // 2) * SLAB, SLAB), SLAB)

    def share_rows(d):
        return pl.ds(pl.multiple_of(d * share, share), share)

    def out_cols(d, t):
        return pl.ds(pl.multiple_of(d * width + t * BLOCK, BLOCK), BLOCK)

    def remote(src, dst, ssem, rsem, k):
        return pltpu.make_async_remote_copy(
            src_ref=src, dst_ref=dst, send_sem=ssem, recv_sem=rsem,
            device_id={"fsdp": peer(k)}, device_id_type=MESH)

    locals_ = [
        pltpu.make_async_copy(grad.at[0], own, loc.at[0]),
        pltpu.make_async_copy(basis.at[:, me // 2, :, lanes_of(me)], hop.at[me], loc.at[1]),
        pltpu.make_async_copy(first.at[0], m1, loc.at[2]),
        pltpu.make_async_copy(second.at[0], m2, loc.at[3]),
    ]
    for t in range(halves):
        locals_.append(pltpu.make_async_copy(
            grad.at[0, :, out_cols(me, t)], got.at[t, share_rows(me)], loc.at[4 + t]))
    for copy in locals_:
        copy.start()

    barrier = pltpu.get_barrier_semaphore()
    for k in range(1, n):
        pl.semaphore_signal(barrier, inc=1, device_id={"fsdp": peer(k)}, device_id_type=MESH)
    for k in range(1, groups):
        pl.semaphore_signal(barrier, inc=1, device_id={"group": zpeer(k)}, device_id_type=MESH)
    pl.semaphore_wait(barrier, n - 1 + groups - 1)

    hops = []
    for k in range(1, n):
        c = peer(k)
        hops.append(remote(basis.at[:, c // 2, :, lanes_of(c)], hop.at[me],
                           hop_s.at[k], hop_r.at[k], k))
        hops[-1].start()

    gots = [[None] * n for _ in range(halves)]

    def send_got(t):
        for k in range(1, n):
            gots[t][k] = remote(grad.at[0, :, out_cols(peer(k), t)], got.at[t, share_rows(me)],
                                got_s.at[t, k], got_r.at[t, k], k)
            gots[t][k].start()

    locals_[0].wait()
    squares = jnp.zeros((8, LANES), jnp.float32)
    for r in range(0, share, 16):
        rows = own[r:r + 16, :].astype(jnp.float32)
        rows = rows * rows
        rows = rows[0:8] + rows[8:16]
        for c in range(0, cols, LANES):
            squares = squares + rows[:, c:c + LANES]
    sq_own[...] = squares
    zs = []
    for k in range(1, groups):
        zs.append(pltpu.make_async_remote_copy(
            src_ref=sq_own, dst_ref=sq_z.at[k], send_sem=z_s.at[k], recv_sem=z_r.at[k],
            device_id={"group": zpeer(k)}, device_id_type=MESH))
        zs[-1].start()

    send_got(0)

    squares = sq_own[...]
    for k, copy in enumerate(zs):
        copy.wait_recv()
        squares = squares + sq_z[k + 1]
    sq_mid[...] = squares
    fs = []
    for k in range(1, n):
        fs.append(remote(sq_mid, sq_f.at[k], f_s.at[k], f_r.at[k], k))
        fs[-1].start()

    for copy in hops:
        copy.wait_recv()
    locals_[1].wait()
    owner = lax.rem(step[0] + ident[0], n)
    for q in range(n):
        staged[q * per_owner:(q + 1) * per_owner] = hop[lax.rem(owner + q, n)]

    rights = [[None] * n for _ in range(halves)]

    def send_right(t):
        for k in range(n):
            d = peer(k)
            src = staged.at[pl.ds(left_groups + (d * halves + t) * block_groups, block_groups)]
            dst = right.at[t, :, rows_of(me), lanes_of(me)]
            if k == 0:
                rights[t][k] = pltpu.make_async_copy(src, dst, right_r.at[t, 0])
            else:
                rights[t][k] = remote(src, dst, right_s.at[t, k], right_r.at[t, k], k)
            rights[t][k].start()

    send_right(0)
    lefts = []
    for k in range(n):
        src = staged.at[pl.ds(0, left_groups)]
        dst = left.at[:, rows_of(me), lanes_of(me)]
        if k == 0:
            lefts.append(pltpu.make_async_copy(src, dst, left_r.at[0]))
        else:
            lefts.append(remote(src, dst, left_s.at[k], left_r.at[k], k))
        lefts[-1].start()
    for t in range(1, halves):
        send_got(t)
        send_right(t)

    squares = sq_mid[...]
    for k, copy in enumerate(fs):
        copy.wait_recv()
        squares = squares + sq_f[k + 1]
    total = jnp.sum(squares, keepdims=True)
    clip = jnp.float32(math.sqrt(entries)) / (jnp.sqrt(total) + 1e-06)
    count = jnp.full((1, 1), step[0].astype(jnp.float32))
    first_inv = 1.0 / (1.0 - jnp.exp(count * jnp.float32(math.log(BETA_ONE))))
    second_inv = 1.0 / (1.0 - jnp.exp(count * jnp.float32(math.log(BETA_TWO))))

    locals_[2].wait()
    locals_[3].wait()
    all_rows = share * n
    left_blocks = all_rows // BLOCK
    returns = []
    outs = []
    for t in range(halves):
        for copy in rights[t][1:]:
            copy.wait_recv()
        rights[t][0].wait()
        if t == 0:
            for copy in lefts[1:]:
                copy.wait_recv()
            lefts[0].wait()
        for k in range(1, n):
            gots[t][k].wait_recv()
        locals_[4 + t].wait()
        rt = right[t].reshape(BLOCK, BLOCK)
        flipped = rt.astype(jnp.float32).T.astype(jnp.bfloat16)
        cut = slice(t * BLOCK, (t + 1) * BLOCK)
        for b in range(left_blocks):
            cols_b = slice(b * BLOCK, (b + 1) * BLOCK)
            lb = left[b * block_groups:(b + 1) * block_groups].reshape(BLOCK, BLOCK)
            turned = mm(flipped, got[t, cols_b, :], NT)
            rotated = sum(mm(piece, lb, NN) for piece in pieces_of(turned)) * clip
            first_sum = BETA_ONE * m1[cut, cols_b].astype(jnp.float32) + (1.0 - BETA_ONE) * rotated
            second_sum = (BETA_TWO * m2[cut, cols_b].astype(jnp.float32)
                          + (1.0 - BETA_TWO) * rotated * rotated)
            n1[cut, cols_b] = first_sum.astype(jnp.bfloat16)
            n2[cut, cols_b] = second_sum.astype(jnp.bfloat16)
            direction = first_sum * first_inv / (jnp.sqrt(second_sum * second_inv) + ADAM_EPS)
            back = sum(mm(rt, piece, NN) for piece in pieces_of(direction))
            result = sum(mm(lb, piece, NT) for piece in pieces_of(back))
            upd[t, cols_b, :] = result.astype(jnp.bfloat16)
        for k in range(n):
            src = upd.at[t, share_rows(peer(k))]
            dst = out_u.at[0, :, out_cols(me, t)]
            if k == 0:
                copy = pltpu.make_async_copy(src, dst, ret_r.at[t, 0])
                outs.append(copy)
            else:
                copy = remote(src, dst, ret_s.at[t, k], ret_r.at[t, k], k)
                returns.append(copy)
            copy.start()
        for index, (value, target) in enumerate(((n1, out_1), (n2, out_2))):
            copy = pltpu.make_async_copy(
                value.at[cut], target.at[0, cut], loc.at[4 + halves + 2 * t + index])
            copy.start()
            outs.append(copy)

    for copy in hops + zs + fs + lefts[1:]:
        copy.wait_send()
    for t in range(halves):
        for k in range(1, n):
            gots[t][k].wait_send()
            rights[t][k].wait_send()
    for copy in outs:
        copy.wait()
    for copy in returns:
        copy.wait()


def hbm(x):
    return pltpu.with_memory_space_constraint(x, pltpu.MemorySpace.HBM)


def copy_kernel(a, b, c, x, y, z, sems):
    copies = [pltpu.make_async_copy(src, dst, sems.at[i])
              for i, (src, dst) in enumerate(((a, x), (b, y), (c, z)))]
    for copy in copies:
        copy.start()
    for copy in copies:
        copy.wait()


def place(arrays):
    return pl.pallas_call(
        copy_kernel,
        out_shape=tuple(jax.ShapeDtypeStruct(a.shape, a.dtype) for a in arrays),
        in_specs=[pl.BlockSpec(memory_space=pltpu.VMEM)] * 3,
        out_specs=(pl.BlockSpec(memory_space=pl.ANY),) * 3,
        scratch_shapes=[pltpu.SemaphoreType.DMA((3,))],
        compiler_params=pltpu.CompilerParams(vmem_limit_bytes=8 << 20),
    )(*arrays)


def fits(gradient, first_moment, basis_store, n):
    if n % 2:
        return False
    span = n // 2 * SLAB
    width = gradient.shape[2] // n
    all_rows = gradient.shape[1] * n
    return (
        BLOCK % span == 0
        and basis_store.shape[1] % span == 0
        and width % BLOCK == 0
        and all_rows % BLOCK == 0
        and gradient.shape[1] % SLAB == 0
        and all_rows <= 1024
        and width <= 1024
    )


def local(gradient, first_moment, second_moment, basis_store, step_number, matrix_ids):
    n = lax.axis_size("fsdp")
    groups = lax.axis_size("group")
    if not fits(gradient, first_moment, basis_store, n):
        return local_general(
            gradient, first_moment, second_moment, basis_store, step_number, matrix_ids
        )
    share, cols = gradient.shape[1:]
    all_rows = share * n
    width = cols // n
    halves = width // BLOCK
    slabs = n // 2
    span = slabs * SLAB
    per_owner = basis_store.shape[1] // span
    basis = basis_store.reshape(per_owner, slabs, SLAB, BLOCK)
    half = jnp.bfloat16
    anywhere = pl.BlockSpec(memory_space=pl.ANY)
    scalar = pl.BlockSpec(memory_space=pltpu.SMEM)
    dma = pltpu.SemaphoreType.DMA
    tile = (8, LANES)
    results = pl.pallas_call(
        functools.partial(kernel, n, groups),
        out_shape=(
            jax.ShapeDtypeStruct(gradient.shape, half),
            jax.ShapeDtypeStruct(first_moment.shape, half),
            jax.ShapeDtypeStruct(second_moment.shape, half),
        ),
        in_specs=[anywhere] * 4 + [scalar] * 2,
        out_specs=(anywhere,) * 3,
        scratch_shapes=[
            pltpu.VMEM((share, cols), half),
            pltpu.VMEM((width, all_rows), half),
            pltpu.VMEM((width, all_rows), half),
            pltpu.VMEM((n, per_owner, SLAB, LANES), half),
            pltpu.VMEM((n * per_owner, SLAB, LANES), half),
            pltpu.VMEM((all_rows // span, span, BLOCK), half),
            pltpu.VMEM((halves, BLOCK // span, span, BLOCK), half),
            pltpu.VMEM((halves, all_rows, BLOCK), half),
            pltpu.VMEM((width, all_rows), half),
            pltpu.VMEM((width, all_rows), half),
            pltpu.VMEM((halves, all_rows, BLOCK), half),
            pltpu.VMEM(tile, jnp.float32),
            pltpu.VMEM((groups,) + tile, jnp.float32),
            pltpu.VMEM(tile, jnp.float32),
            pltpu.VMEM((n,) + tile, jnp.float32),
            dma((4 + 3 * halves,)),
            dma((n,)), dma((n,)),
            dma((n,)), dma((n,)),
            dma((halves, n)), dma((halves, n)),
            dma((halves, n)), dma((halves, n)),
            dma((halves, n)), dma((halves, n)),
            dma((groups,)), dma((groups,)),
            dma((n,)), dma((n,)),
        ],
        compiler_params=pltpu.CompilerParams(
            collective_id=0, has_side_effects=True, vmem_limit_bytes=32 << 20
        ),
    )(*[hbm(x) for x in (gradient, first_moment, second_moment, basis)], step_number, matrix_ids)
    return place(results)


def solution(mesh):
    in_specs = (
        P("group", "fsdp", None),
        P("group", "fsdp", None),
        P("group", "fsdp", None),
        P("group", "fsdp", None),
        P(),
        P("group"),
    )
    out_specs = (P("group", "fsdp", None), P("group", "fsdp", None), P("group", "fsdp", None))
    return jax.shard_map(local, mesh=mesh, in_specs=in_specs, out_specs=out_specs, check_vma=False)
```

```python
import functools
import math

import jax
import jax.numpy as jnp
from jax import lax
from jax.experimental import pallas as pl
from jax.experimental.pallas import tpu as pltpu
from jax.sharding import PartitionSpec as P

BLOCK = 256


BETA_ONE = 0.95
BETA_TWO = 0.95
ADAM_EPS = 1e-08
HIGHEST = lax.Precision.HIGHEST


def clip_of(local_squares, entries):
    total = lax.psum(local_squares, ("fsdp", "group"))
    return jnp.float32(math.sqrt(entries)) / (jnp.sqrt(total) + 1e-06)


def local_general(gradient, first_moment, second_moment, basis_store, step_number, matrix_ids):
    fsdp_count = lax.axis_size("fsdp")
    group_count = lax.axis_size("group")
    row_count = gradient.shape[1]
    col_count = gradient.shape[2]
    all_rows = row_count * fsdp_count
    col_share = col_count // fsdp_count
    left_blocks = all_rows // BLOCK
    right_blocks = col_count // BLOCK
    entries = all_rows * col_count * group_count
    grad_local = gradient[0].astype(jnp.float32)
    local_squares = jnp.sum(grad_local * grad_local)
    gathered = lax.all_gather(basis_store[0], "fsdp", axis=0, tiled=True)
    owner_rows = basis_store.shape[1]
    owner = (step_number[0] + matrix_ids[0]) % fsdp_count
    ordered_half = jnp.roll(gathered, -owner * owner_rows, axis=0)
    left = ordered_half[:all_rows].astype(jnp.float32).reshape(left_blocks, BLOCK, BLOCK)
    right_half = ordered_half[all_rows:].reshape(right_blocks, BLOCK, BLOCK)
    right = right_half.astype(jnp.float32)
    turned = jnp.einsum(
        "rbj,bjl->rbl",
        gradient[0].reshape(row_count, right_blocks, BLOCK),
        right_half,
        preferred_element_type=jnp.float32,
    )
    turned = clip_of(local_squares, entries) * turned
    outgoing = turned.reshape(row_count, fsdp_count, col_share)
    received = lax.all_to_all(outgoing, "fsdp", split_axis=1, concat_axis=0, tiled=True)
    width = received.shape[2]
    columns = received[:, 0, :].reshape(left_blocks, BLOCK, width)
    rotated = jnp.einsum("bkc,bki->cbi", columns, left, precision=HIGHEST).reshape(width, all_rows)
    count = step_number[0].astype(jnp.float32)
    first_fix = 1.0 - jnp.power(jnp.float32(BETA_ONE), count)
    second_fix = 1.0 - jnp.power(jnp.float32(BETA_TWO), count)
    first_sum = BETA_ONE * first_moment[0].astype(jnp.float32) + (1.0 - BETA_ONE) * rotated
    second_sum = (
        BETA_TWO * second_moment[0].astype(jnp.float32) + (1.0 - BETA_TWO) * rotated * rotated
    )
    direction = first_sum / first_fix / (jnp.sqrt(second_sum / second_fix) + ADAM_EPS)
    backward = jnp.einsum(
        "cbi,bki->cbk", direction.reshape(col_share, left_blocks, BLOCK), left, precision=HIGHEST
    )
    returning = backward.reshape(col_share, fsdp_count, row_count)
    received = lax.all_to_all(returning, "fsdp", split_axis=1, concat_axis=0, tiled=True)
    width = received.shape[2]
    pieces = received[:, 0, :].reshape(right_blocks, BLOCK, width)
    result = jnp.einsum("blr,bjl->rbj", pieces, right, precision=HIGHEST).reshape(width, col_count)
    return (
        result[None].astype(jnp.bfloat16),
        first_sum[None].astype(jnp.bfloat16),
        second_sum[None].astype(jnp.bfloat16),
    )


SLAB = 16
LANES = 128
PARTS = 1
MESH = pl.DeviceIdType.MESH


def pieces_of(x):
    high = x.astype(jnp.bfloat16)
    rest = x - high.astype(jnp.float32)
    middle = rest.astype(jnp.bfloat16)
    low = (rest - middle.astype(jnp.float32)).astype(jnp.bfloat16)
    return high, middle, low


def mm(a, b, dims):
    return lax.dot_general(a, b, (dims, ((), ())), preferred_element_type=jnp.float32)


NN = ((1,), (0,))
NT = ((1,), (1,))


def kernel(n, groups, grad, first, second, basis, step, ident, out_u, out_1, out_2,
           own, m1, m2, hop, staged, left, right, got, n1, n2, upd, sq_own, sq_z, sq_mid, sq_f,
           loc, hop_s, hop_r, left_s, left_r, right_s, right_r, got_s, got_r,
           ret_s, ret_r, z_s, z_r, f_s, f_r):
    me = lax.axis_index("fsdp")
    zz = lax.axis_index("group")
    share = grad.shape[1]
    cols = grad.shape[2]
    width = cols // n
    halves = width // BLOCK
    slabs = n // 2
    per_owner = basis.shape[0]
    span = slabs * SLAB
    left_groups = left.shape[0]
    all_rows = share * n
    left_blocks = all_rows // BLOCK
    block_groups = BLOCK // span
    entries = float(share * n * cols * groups)

    core = lax.rem(me, 2)
    per = n // left_blocks
    masks = [m for m in range(2, n, 2)] + [m for m in range(3, n, 2)]
    swapped = [masks[i + 1] if i % 2 == 0 and i + 1 < len(masks) else masks[i - i % 2] for i in range(len(masks))]
    order = list(zip(masks, swapped)) + [(1, 1)]

    def peer(m):
        other = me
        for bit in (1 << i for i in range(n.bit_length() - 1)):
            if m & bit:
                other = other + bit * (1 - 2 * lax.rem(me // bit, 2))
        return other

    def pick(pair):
        a, b = pair
        return a + core * (b - a), peer(a) + core * (peer(b) - peer(a))

    def zpeer(k):
        return lax.rem(zz + k, groups)

    def lanes_of(c):
        return pl.ds(pl.multiple_of(lax.rem(c, 2) * LANES, LANES), LANES)

    def rows_of(c):
        return pl.ds(pl.multiple_of((c // 2) * SLAB, SLAB), SLAB)

    def share_rows(d):
        return pl.ds(pl.multiple_of(d * share, share), share)

    def out_cols(d, t):
        return pl.ds(pl.multiple_of(d * width + t * BLOCK, BLOCK), BLOCK)

    def remote(src, dst, ssem, rsem, d):
        return pltpu.make_async_remote_copy(
            src_ref=src, dst_ref=dst, send_sem=ssem, recv_sem=rsem,
            device_id={"fsdp": d}, device_id_type=MESH)

    locals_ = [
        pltpu.make_async_copy(grad.at[0], own, loc.at[0]),
        pltpu.make_async_copy(basis.at[:, me // 2, :, lanes_of(me)], hop.at[me], loc.at[1]),
        pltpu.make_async_copy(first.at[0], m1, loc.at[2]),
        pltpu.make_async_copy(second.at[0], m2, loc.at[3]),
    ]
    for t in range(halves):
        locals_.append(pltpu.make_async_copy(
            grad.at[0, :, out_cols(me, t)], got.at[t, share_rows(me)], loc.at[4 + t]))
    for copy in locals_:
        copy.start()

    barrier = pltpu.get_barrier_semaphore()
    for k in range(1, n):
        pl.semaphore_signal(barrier, inc=1, device_id={"fsdp": peer(k)}, device_id_type=MESH)
    for k in range(1, groups):
        pl.semaphore_signal(barrier, inc=1, device_id={"group": zpeer(k)}, device_id_type=MESH)
    pl.semaphore_wait(barrier, n - 1 + groups - 1)

    def hop_copy(m, d):
        return remote(basis.at[:, d // 2, :, lanes_of(d)], hop.at[me], hop_s.at[m], hop_r.at[m], d)

    def got_copy(t, m, d):
        return remote(grad.at[0, :, out_cols(d, t)], got.at[t, share_rows(me)],
                      got_s.at[t, m], got_r.at[t, m], d)

    def right_copy(t, m, d):
        src = staged.at[pl.ds(left_groups + (d * halves + t) * block_groups, block_groups)]
        dst = right.at[t, :, rows_of(me), lanes_of(me)]
        return remote(src, dst, right_s.at[t, m], right_r.at[t, m], d)

    def left_copy(m, d):
        return remote(staged.at[pl.ds(0, left_groups)], left.at[:, rows_of(me), lanes_of(me)],
                      left_s.at[m], left_r.at[m], d)

    for pair in order:
        hop_copy(*pick(pair)).start()
    hops = [hop_copy(m, peer(m)) for m in range(1, n)]
    gots = [[None] + [got_copy(t, m, peer(m)) for m in range(1, n)] for t in range(halves)]
    rights = [[None] + [right_copy(t, m, peer(m)) for m in range(1, n)] for t in range(halves)]
    lefts = [left_copy(m, peer(m)) for m in range(2, n, 2)]
    shared = left.at[:, :, lanes_of(me)]
    sibling = remote(shared, shared, left_s.at[1], left_r.at[1], peer(1))

    def send_got(t):
        for pair in order:
            got_copy(t, *pick(pair)).start()

    locals_[0].wait()
    squares = jnp.zeros((8, LANES), jnp.float32)
    for r in range(0, share, 16):
        rows = own[r:r + 16, :].astype(jnp.float32)
        rows = rows * rows
        rows = rows[0:8] + rows[8:16]
        for c in range(0, cols, LANES):
            squares = squares + rows[:, c:c + LANES]
    sq_own[...] = squares
    zs = []
    for k in range(1, groups):
        zs.append(pltpu.make_async_remote_copy(
            src_ref=sq_own, dst_ref=sq_z.at[k], send_sem=z_s.at[k], recv_sem=z_r.at[k],
            device_id={"group": zpeer(k)}, device_id_type=MESH))
        zs[-1].start()

    send_got(0)

    squares = sq_own[...]
    for k, copy in enumerate(zs):
        copy.wait_recv()
        squares = squares + sq_z[k + 1]
    sq_mid[...] = squares
    fs = []
    for k in range(1, n):
        fs.append(remote(sq_mid, sq_f.at[k], f_s.at[k], f_r.at[k], peer(k)))
        fs[-1].start()

    for copy in hops:
        copy.wait_recv()
    locals_[1].wait()
    owner = lax.rem(step[0] + ident[0], n)
    for q in range(n):
        staged[q * per_owner:(q + 1) * per_owner] = hop[lax.rem(owner + q, n)]

    own_left = pltpu.make_async_copy(
        staged.at[pl.ds(0, left_groups)], left.at[:, rows_of(me), lanes_of(me)], left_r.at[0])
    own_left.start()
    own_rights = [pltpu.make_async_copy(
        staged.at[pl.ds(left_groups + (me * halves + t) * block_groups, block_groups)],
        right.at[t, :, rows_of(me), lanes_of(me)], right_r.at[t, 0]) for t in range(halves)]
    for copy in own_rights:
        copy.start()
    lefts_order = [m for m in order if m[0] % 2 == 0]
    for m, _ in lefts_order:
        left_copy(m, peer(m)).start()

    def send_right(t):
        for pair in order:
            right_copy(t, *pick(pair)).start()

    send_right(0)
    for t in range(1, halves):
        send_got(t)
        send_right(t)

    squares = sq_mid[...]
    for k, copy in enumerate(fs):
        copy.wait_recv()
        squares = squares + sq_f[k + 1]
    total = jnp.sum(squares, keepdims=True)
    clip = jnp.float32(math.sqrt(entries)) / (jnp.sqrt(total) + 1e-06)
    count = jnp.full((1, 1), step[0].astype(jnp.float32))
    first_inv = 1.0 / (1.0 - jnp.exp(count * jnp.float32(math.log(BETA_ONE))))
    second_inv = 1.0 / (1.0 - jnp.exp(count * jnp.float32(math.log(BETA_TWO))))

    locals_[2].wait()
    locals_[3].wait()
    returns = []
    outs = []
    for copy in lefts:
        copy.wait_recv()
    own_left.wait()
    sibling.start()
    for t in range(halves):
        for copy in rights[t][1:]:
            copy.wait_recv()
        own_rights[t].wait()
        rt = right[t].reshape(BLOCK, BLOCK)
        flipped = rt.astype(jnp.float32).T.astype(jnp.bfloat16)
        cut = slice(t * BLOCK, (t + 1) * BLOCK)
        if t == 0:
            sibling.wait_recv()
        for i in reversed(range(left_blocks)):
            b = peer(i * per) // per
            cols_b = pl.ds(pl.multiple_of(b * BLOCK, BLOCK), BLOCK)
            near = range(i * per, (i + 1) * per)
            for m in near:
                if m:
                    gots[t][m].wait_recv()
                else:
                    locals_[4 + t].wait()
            lb = left[pl.ds(b * block_groups, block_groups)].reshape(BLOCK, BLOCK)
            turned = mm(flipped, got[t, cols_b, :], NT)
            rotated = sum(mm(piece, lb, NN) for piece in pieces_of(turned)) * clip
            first_sum = BETA_ONE * m1[cut, cols_b].astype(jnp.float32) + (1.0 - BETA_ONE) * rotated
            second_sum = (BETA_TWO * m2[cut, cols_b].astype(jnp.float32)
                          + (1.0 - BETA_TWO) * rotated * rotated)
            n1[cut, cols_b] = first_sum.astype(jnp.bfloat16)
            n2[cut, cols_b] = second_sum.astype(jnp.bfloat16)
            direction = first_sum * first_inv / (jnp.sqrt(second_sum * second_inv) + ADAM_EPS)
            back = sum(mm(rt, piece, NN) for piece in pieces_of(direction))
            result = sum(mm(lb, piece, NT) for piece in pieces_of(back))
            upd[t, cols_b, :] = result.astype(jnp.bfloat16)
            for m in reversed(near):
                src = upd.at[t, share_rows(peer(m))]
                dst = out_u.at[0, :, out_cols(me, t)]
                if m == 0:
                    copy = pltpu.make_async_copy(src, dst, ret_r.at[t, 0])
                    outs.append(copy)
                else:
                    copy = remote(src, dst, ret_s.at[t, m], ret_r.at[t, m], peer(m))
                    returns.append(copy)
                copy.start()
        for index, (value, target) in enumerate(((n1, out_1), (n2, out_2))):
            copy = pltpu.make_async_copy(
                value.at[cut], target.at[0, cut], loc.at[4 + halves + 2 * t + index])
            copy.start()
            outs.append(copy)

    for copy in hops + zs + fs + lefts + [sibling]:
        copy.wait_send()
    for t in range(halves):
        for m in range(1, n):
            gots[t][m].wait_send()
            rights[t][m].wait_send()
    for copy in outs:
        copy.wait()
    for copy in returns:
        copy.wait()


def hbm(x):
    return pltpu.with_memory_space_constraint(x, pltpu.MemorySpace.HBM)


def copy_kernel(a, b, c, x, y, z, sems):
    copies = []
    for src, dst in ((a, x), (b, y), (c, z)):
        rows = src.shape[1] // PARTS
        for i in range(PARTS):
            cut = pl.ds(i * rows, rows)
            copies.append(pltpu.make_async_copy(
                src.at[0, cut], dst.at[0, cut], sems.at[len(copies)]))
    for copy in copies:
        copy.start()
    for copy in copies:
        copy.wait()


def place(arrays):
    return pl.pallas_call(
        copy_kernel,
        out_shape=tuple(jax.ShapeDtypeStruct(a.shape, a.dtype) for a in arrays),
        in_specs=[pl.BlockSpec(memory_space=pltpu.VMEM)] * 3,
        out_specs=(pl.BlockSpec(memory_space=pl.ANY),) * 3,
        scratch_shapes=[pltpu.SemaphoreType.DMA((3 * PARTS,))],
        compiler_params=pltpu.CompilerParams(vmem_limit_bytes=8 << 20),
    )(*arrays)


def fits(gradient, first_moment, basis_store, n):
    if n < 2 or n & (n - 1):
        return False
    span = n // 2 * SLAB
    width = gradient.shape[2] // n
    all_rows = gradient.shape[1] * n
    return (
        BLOCK % span == 0
        and basis_store.shape[1] % span == 0
        and width % BLOCK == 0
        and all_rows % BLOCK == 0
        and n % (all_rows // BLOCK) == 0
        and gradient.shape[1] % SLAB == 0
        and all_rows <= 1024
        and width <= 1024
    )


def local(gradient, first_moment, second_moment, basis_store, step_number, matrix_ids):
    n = lax.axis_size("fsdp")
    groups = lax.axis_size("group")
    if not fits(gradient, first_moment, basis_store, n):
        return local_general(
            gradient, first_moment, second_moment, basis_store, step_number, matrix_ids
        )
    share, cols = gradient.shape[1:]
    all_rows = share * n
    width = cols // n
    halves = width // BLOCK
    slabs = n // 2
    span = slabs * SLAB
    per_owner = basis_store.shape[1] // span
    basis = basis_store.reshape(per_owner, slabs, SLAB, BLOCK)
    half = jnp.bfloat16
    anywhere = pl.BlockSpec(memory_space=pl.ANY)
    scalar = pl.BlockSpec(memory_space=pltpu.SMEM)
    dma = pltpu.SemaphoreType.DMA
    tile = (8, LANES)
    results = pl.pallas_call(
        functools.partial(kernel, n, groups),
        out_shape=(
            jax.ShapeDtypeStruct(gradient.shape, half),
            jax.ShapeDtypeStruct(first_moment.shape, half),
            jax.ShapeDtypeStruct(second_moment.shape, half),
        ),
        in_specs=[anywhere] * 4 + [scalar] * 2,
        out_specs=(anywhere,) * 3,
        scratch_shapes=[
            pltpu.VMEM((share, cols), half),
            pltpu.VMEM((width, all_rows), half),
            pltpu.VMEM((width, all_rows), half),
            pltpu.VMEM((n, per_owner, SLAB, LANES), half),
            pltpu.VMEM((n * per_owner, SLAB, LANES), half),
            pltpu.VMEM((all_rows // span, span, BLOCK), half),
            pltpu.VMEM((halves, BLOCK // span, span, BLOCK), half),
            pltpu.VMEM((halves, all_rows, BLOCK), half),
            pltpu.VMEM((width, all_rows), half),
            pltpu.VMEM((width, all_rows), half),
            pltpu.VMEM((halves, all_rows, BLOCK), half),
            pltpu.VMEM(tile, jnp.float32),
            pltpu.VMEM((groups,) + tile, jnp.float32),
            pltpu.VMEM(tile, jnp.float32),
            pltpu.VMEM((n,) + tile, jnp.float32),
            dma((4 + 3 * halves,)),
            dma((n,)), dma((n,)),
            dma((n,)), dma((n,)),
            dma((halves, n)), dma((halves, n)),
            dma((halves, n)), dma((halves, n)),
            dma((halves, n)), dma((halves, n)),
            dma((groups,)), dma((groups,)),
            dma((n,)), dma((n,)),
        ],
        compiler_params=pltpu.CompilerParams(
            collective_id=0, has_side_effects=True, vmem_limit_bytes=32 << 20
        ),
    )(*[hbm(x) for x in (gradient, first_moment, second_moment, basis)], step_number, matrix_ids)
    return place(results)


def solution(mesh):
    in_specs = (
        P("group", "fsdp", None),
        P("group", "fsdp", None),
        P("group", "fsdp", None),
        P("group", "fsdp", None),
        P(),
        P("group"),
    )
    out_specs = (P("group", "fsdp", None), P("group", "fsdp", None), P("group", "fsdp", None))
    return jax.shard_map(local, mesh=mesh, in_specs=in_specs, out_specs=out_specs, check_vma=False)
```

```python
import functools
import math

import jax
import jax.numpy as jnp
from jax import lax
from jax.experimental import pallas as pl
from jax.experimental.pallas import tpu as pltpu
from jax.sharding import PartitionSpec as P

BLOCK = 256


BETA_ONE = 0.95
BETA_TWO = 0.95
ADAM_EPS = 1e-08
HIGHEST = lax.Precision.HIGHEST


def clip_of(local_squares, entries):
    total = lax.psum(local_squares, ("fsdp", "group"))
    return jnp.float32(math.sqrt(entries)) / (jnp.sqrt(total) + 1e-06)


def local_general(gradient, first_moment, second_moment, basis_store, step_number, matrix_ids):
    fsdp_count = lax.axis_size("fsdp")
    group_count = lax.axis_size("group")
    row_count = gradient.shape[1]
    col_count = gradient.shape[2]
    all_rows = row_count * fsdp_count
    col_share = col_count // fsdp_count
    left_blocks = all_rows // BLOCK
    right_blocks = col_count // BLOCK
    entries = all_rows * col_count * group_count
    grad_local = gradient[0].astype(jnp.float32)
    local_squares = jnp.sum(grad_local * grad_local)
    gathered = lax.all_gather(basis_store[0], "fsdp", axis=0, tiled=True)
    owner_rows = basis_store.shape[1]
    owner = (step_number[0] + matrix_ids[0]) % fsdp_count
    ordered_half = jnp.roll(gathered, -owner * owner_rows, axis=0)
    left = ordered_half[:all_rows].astype(jnp.float32).reshape(left_blocks, BLOCK, BLOCK)
    right_half = ordered_half[all_rows:].reshape(right_blocks, BLOCK, BLOCK)
    right = right_half.astype(jnp.float32)
    turned = jnp.einsum(
        "rbj,bjl->rbl",
        gradient[0].reshape(row_count, right_blocks, BLOCK),
        right_half,
        preferred_element_type=jnp.float32,
    )
    turned = clip_of(local_squares, entries) * turned
    outgoing = turned.reshape(row_count, fsdp_count, col_share)
    received = lax.all_to_all(outgoing, "fsdp", split_axis=1, concat_axis=0, tiled=True)
    width = received.shape[2]
    columns = received[:, 0, :].reshape(left_blocks, BLOCK, width)
    rotated = jnp.einsum("bkc,bki->cbi", columns, left, precision=HIGHEST).reshape(width, all_rows)
    count = step_number[0].astype(jnp.float32)
    first_fix = 1.0 - jnp.power(jnp.float32(BETA_ONE), count)
    second_fix = 1.0 - jnp.power(jnp.float32(BETA_TWO), count)
    first_sum = BETA_ONE * first_moment[0].astype(jnp.float32) + (1.0 - BETA_ONE) * rotated
    second_sum = (
        BETA_TWO * second_moment[0].astype(jnp.float32) + (1.0 - BETA_TWO) * rotated * rotated
    )
    direction = first_sum / first_fix / (jnp.sqrt(second_sum / second_fix) + ADAM_EPS)
    backward = jnp.einsum(
        "cbi,bki->cbk", direction.reshape(col_share, left_blocks, BLOCK), left, precision=HIGHEST
    )
    returning = backward.reshape(col_share, fsdp_count, row_count)
    received = lax.all_to_all(returning, "fsdp", split_axis=1, concat_axis=0, tiled=True)
    width = received.shape[2]
    pieces = received[:, 0, :].reshape(right_blocks, BLOCK, width)
    result = jnp.einsum("blr,bjl->rbj", pieces, right, precision=HIGHEST).reshape(width, col_count)
    return (
        result[None].astype(jnp.bfloat16),
        first_sum[None].astype(jnp.bfloat16),
        second_sum[None].astype(jnp.bfloat16),
    )


SLAB = 16
LANES = 128
PARTS = 1
MESH = pl.DeviceIdType.MESH


def pieces_of(x):
    high = x.astype(jnp.bfloat16)
    rest = x - high.astype(jnp.float32)
    middle = rest.astype(jnp.bfloat16)
    low = (rest - middle.astype(jnp.float32)).astype(jnp.bfloat16)
    return high, middle, low


def mm(a, b, dims):
    return lax.dot_general(a, b, (dims, ((), ())), preferred_element_type=jnp.float32)


NN = ((1,), (0,))
NT = ((1,), (1,))


def kernel(n, groups, grad, first, second, basis, step, ident, out_u, out_1, out_2,
           own, m1, m2, hop, staged, left, right, got, n1, n2, upd, sq_own, sq_z, sq_mid, sq_f,
           loc, hop_s, hop_r, left_s, left_r, right_s, right_r, got_s, got_r,
           ret_s, ret_r, z_s, z_r, f_s, f_r):
    me = lax.axis_index("fsdp")
    zz = lax.axis_index("group")
    share = grad.shape[1]
    cols = grad.shape[2]
    width = cols // n
    halves = width // BLOCK
    slabs = n // 2
    per_owner = basis.shape[0]
    span = slabs * SLAB
    left_groups = left.shape[0]
    all_rows = share * n
    left_blocks = all_rows // BLOCK
    block_groups = BLOCK // span
    entries = float(share * n * cols * groups)

    core = lax.rem(me, 2)
    per = n // left_blocks
    masks = [m for m in range(2, n, 2)] + [m for m in range(3, n, 2)]
    swapped = [masks[i + 1] if i % 2 == 0 and i + 1 < len(masks) else masks[i - i % 2] for i in range(len(masks))]
    order = list(zip(masks, swapped)) + [(1, 1)]

    def peer(m):
        other = me
        for bit in (1 << i for i in range(n.bit_length() - 1)):
            if m & bit:
                other = other + bit * (1 - 2 * lax.rem(me // bit, 2))
        return other

    def pick(pair):
        a, b = pair
        return a + core * (b - a), peer(a) + core * (peer(b) - peer(a))

    def zpeer(k):
        return lax.rem(zz + k, groups)

    def lanes_of(c):
        return pl.ds(pl.multiple_of(lax.rem(c, 2) * LANES, LANES), LANES)

    def rows_of(c):
        return pl.ds(pl.multiple_of((c // 2) * SLAB, SLAB), SLAB)

    def share_rows(d):
        return pl.ds(pl.multiple_of(d * share, share), share)

    def out_cols(d, t):
        return pl.ds(pl.multiple_of(d * width + t * BLOCK, BLOCK), BLOCK)

    def remote(src, dst, ssem, rsem, d):
        return pltpu.make_async_remote_copy(
            src_ref=src, dst_ref=dst, send_sem=ssem, recv_sem=rsem,
            device_id={"fsdp": d}, device_id_type=MESH)

    locals_ = [
        pltpu.make_async_copy(grad.at[0], own, loc.at[0]),
        pltpu.make_async_copy(basis.at[:, me // 2, :, lanes_of(me)], hop.at[me], loc.at[1]),
        pltpu.make_async_copy(first.at[0], m1, loc.at[2]),
        pltpu.make_async_copy(second.at[0], m2, loc.at[3]),
    ]
    for t in range(halves):
        locals_.append(pltpu.make_async_copy(
            grad.at[0, :, out_cols(me, t)], got.at[t, share_rows(me)], loc.at[4 + t]))
    for copy in locals_:
        copy.start()

    barrier = pltpu.get_barrier_semaphore()
    for k in range(1, n):
        pl.semaphore_signal(barrier, inc=1, device_id={"fsdp": peer(k)}, device_id_type=MESH)
    for k in range(1, groups):
        pl.semaphore_signal(barrier, inc=1, device_id={"group": zpeer(k)}, device_id_type=MESH)
    pl.semaphore_wait(barrier, n - 1 + groups - 1)

    def hop_copy(m, d):
        return remote(basis.at[:, d // 2, :, lanes_of(d)], hop.at[me], hop_s.at[m], hop_r.at[m], d)

    def got_copy(t, m, d):
        return remote(own.at[:, out_cols(d, t)], got.at[t, share_rows(me)],
                      got_s.at[t, m], got_r.at[t, m], d)

    def right_copy(t, m, d):
        src = staged.at[pl.ds(left_groups + (d * halves + t) * block_groups, block_groups)]
        dst = right.at[t, :, rows_of(me), lanes_of(me)]
        return remote(src, dst, right_s.at[t, m], right_r.at[t, m], d)

    def left_copy(m, d):
        return remote(staged.at[pl.ds(0, left_groups)], left.at[:, rows_of(me), lanes_of(me)],
                      left_s.at[m], left_r.at[m], d)

    for pair in order:
        hop_copy(*pick(pair)).start()
    hops = [hop_copy(m, peer(m)) for m in range(1, n)]
    gots = [[None] + [got_copy(t, m, peer(m)) for m in range(1, n)] for t in range(halves)]
    rights = [[None] + [right_copy(t, m, peer(m)) for m in range(1, n)] for t in range(halves)]
    lefts = [left_copy(m, peer(m)) for m in range(2, n, 2)]
    shared = left.at[:, :, lanes_of(me)]
    sibling = remote(shared, shared, left_s.at[1], left_r.at[1], peer(1))

    def send_got(t):
        for pair in order:
            got_copy(t, *pick(pair)).start()

    locals_[0].wait()
    squares = jnp.zeros((8, LANES), jnp.float32)
    for r in range(0, share, 16):
        rows = own[r:r + 16, :].astype(jnp.float32)
        rows = rows * rows
        rows = rows[0:8] + rows[8:16]
        for c in range(0, cols, LANES):
            squares = squares + rows[:, c:c + LANES]
    sq_own[...] = squares
    zs = []
    for k in range(1, groups):
        zs.append(pltpu.make_async_remote_copy(
            src_ref=sq_own, dst_ref=sq_z.at[k], send_sem=z_s.at[k], recv_sem=z_r.at[k],
            device_id={"group": zpeer(k)}, device_id_type=MESH))
        zs[-1].start()

    send_got(0)

    squares = sq_own[...]
    for k, copy in enumerate(zs):
        copy.wait_recv()
        squares = squares + sq_z[k + 1]
    sq_mid[...] = squares
    fs = []
    for k in range(1, n):
        fs.append(remote(sq_mid, sq_f.at[k], f_s.at[k], f_r.at[k], peer(k)))
        fs[-1].start()

    for copy in hops:
        copy.wait_recv()
    locals_[1].wait()
    owner = lax.rem(step[0] + ident[0], n)
    for q in range(n):
        staged[q * per_owner:(q + 1) * per_owner] = hop[lax.rem(owner + q, n)]

    own_left = pltpu.make_async_copy(
        staged.at[pl.ds(0, left_groups)], left.at[:, rows_of(me), lanes_of(me)], left_r.at[0])
    own_left.start()
    own_rights = [pltpu.make_async_copy(
        staged.at[pl.ds(left_groups + (me * halves + t) * block_groups, block_groups)],
        right.at[t, :, rows_of(me), lanes_of(me)], right_r.at[t, 0]) for t in range(halves)]
    for copy in own_rights:
        copy.start()
    lefts_order = [m for m in order if m[0] % 2 == 0]
    def send_right(t):
        for pair in order:
            right_copy(t, *pick(pair)).start()

    send_right(0)
    for m, _ in lefts_order:
        left_copy(m, peer(m)).start()
    for t in range(1, halves):
        send_right(t)
        send_got(t)

    squares = sq_mid[...]
    for k, copy in enumerate(fs):
        copy.wait_recv()
        squares = squares + sq_f[k + 1]
    total = jnp.sum(squares, keepdims=True)
    clip = jnp.float32(math.sqrt(entries)) / (jnp.sqrt(total) + 1e-06)
    count = jnp.full((1, 1), step[0].astype(jnp.float32))
    first_inv = 1.0 / (1.0 - jnp.exp(count * jnp.float32(math.log(BETA_ONE))))
    second_inv = 1.0 / (1.0 - jnp.exp(count * jnp.float32(math.log(BETA_TWO))))

    locals_[2].wait()
    locals_[3].wait()
    returns = []
    outs = []
    for copy in lefts:
        copy.wait_recv()
    own_left.wait()
    sibling.start()
    for t in range(halves):
        for copy in rights[t][1:]:
            copy.wait_recv()
        own_rights[t].wait()
        rt = right[t].reshape(BLOCK, BLOCK)
        flipped = rt.astype(jnp.float32).T.astype(jnp.bfloat16)
        cut = slice(t * BLOCK, (t + 1) * BLOCK)
        if t == 0:
            sibling.wait_recv()
        for i in reversed(range(left_blocks)):
            b = peer(i * per) // per
            cols_b = pl.ds(pl.multiple_of(b * BLOCK, BLOCK), BLOCK)
            near = range(i * per, (i + 1) * per)
            for m in near:
                if m:
                    gots[t][m].wait_recv()
                else:
                    locals_[4 + t].wait()
            lb = left[pl.ds(b * block_groups, block_groups)].reshape(BLOCK, BLOCK)
            turned = mm(flipped, got[t, cols_b, :], NT)
            rotated = sum(mm(piece, lb, NN) for piece in pieces_of(turned)) * clip
            first_sum = BETA_ONE * m1[cut, cols_b].astype(jnp.float32) + (1.0 - BETA_ONE) * rotated
            second_sum = (BETA_TWO * m2[cut, cols_b].astype(jnp.float32)
                          + (1.0 - BETA_TWO) * rotated * rotated)
            n1[cut, cols_b] = first_sum.astype(jnp.bfloat16)
            n2[cut, cols_b] = second_sum.astype(jnp.bfloat16)
            direction = first_sum * first_inv / (jnp.sqrt(second_sum * second_inv) + ADAM_EPS)
            back = sum(mm(rt, piece, NN) for piece in pieces_of(direction))
            result = sum(mm(lb, piece, NT) for piece in pieces_of(back))
            upd[t, cols_b, :] = result.astype(jnp.bfloat16)
            for m in reversed(near):
                src = upd.at[t, share_rows(peer(m))]
                dst = out_u.at[0, :, out_cols(me, t)]
                if m == 0:
                    copy = pltpu.make_async_copy(src, dst, ret_r.at[t, 0])
                    outs.append(copy)
                else:
                    copy = remote(src, dst, ret_s.at[t, m], ret_r.at[t, m], peer(m))
                    returns.append(copy)
                copy.start()
        for index, (value, target) in enumerate(((n1, out_1), (n2, out_2))):
            copy = pltpu.make_async_copy(
                value.at[cut], target.at[0, cut], loc.at[4 + halves + 2 * t + index])
            copy.start()
            outs.append(copy)

    for copy in hops + zs + fs + lefts + [sibling]:
        copy.wait_send()
    for t in range(halves):
        for m in range(1, n):
            gots[t][m].wait_send()
            rights[t][m].wait_send()
    for copy in outs:
        copy.wait()
    for copy in returns:
        copy.wait()


def hbm(x):
    return pltpu.with_memory_space_constraint(x, pltpu.MemorySpace.HBM)


def copy_kernel(a, b, c, x, y, z, sems):
    copies = []
    for src, dst in ((a, x), (b, y), (c, z)):
        rows = src.shape[1] // PARTS
        for i in range(PARTS):
            cut = pl.ds(i * rows, rows)
            copies.append(pltpu.make_async_copy(
                src.at[0, cut], dst.at[0, cut], sems.at[len(copies)]))
    for copy in copies:
        copy.start()
    for copy in copies:
        copy.wait()


def place(arrays):
    return pl.pallas_call(
        copy_kernel,
        out_shape=tuple(jax.ShapeDtypeStruct(a.shape, a.dtype) for a in arrays),
        in_specs=[pl.BlockSpec(memory_space=pltpu.VMEM)] * 3,
        out_specs=(pl.BlockSpec(memory_space=pl.ANY),) * 3,
        scratch_shapes=[pltpu.SemaphoreType.DMA((3 * PARTS,))],
        compiler_params=pltpu.CompilerParams(vmem_limit_bytes=8 << 20),
    )(*arrays)


def fits(gradient, first_moment, basis_store, n):
    if n < 2 or n & (n - 1):
        return False
    span = n // 2 * SLAB
    width = gradient.shape[2] // n
    all_rows = gradient.shape[1] * n
    return (
        BLOCK % span == 0
        and basis_store.shape[1] % span == 0
        and width % BLOCK == 0
        and all_rows % BLOCK == 0
        and n % (all_rows // BLOCK) == 0
        and gradient.shape[1] % SLAB == 0
        and all_rows <= 1024
        and width <= 1024
    )


def local(gradient, first_moment, second_moment, basis_store, step_number, matrix_ids):
    n = lax.axis_size("fsdp")
    groups = lax.axis_size("group")
    if not fits(gradient, first_moment, basis_store, n):
        return local_general(
            gradient, first_moment, second_moment, basis_store, step_number, matrix_ids
        )
    share, cols = gradient.shape[1:]
    all_rows = share * n
    width = cols // n
    halves = width // BLOCK
    slabs = n // 2
    span = slabs * SLAB
    per_owner = basis_store.shape[1] // span
    basis = basis_store.reshape(per_owner, slabs, SLAB, BLOCK)
    half = jnp.bfloat16
    anywhere = pl.BlockSpec(memory_space=pl.ANY)
    scalar = pl.BlockSpec(memory_space=pltpu.SMEM)
    dma = pltpu.SemaphoreType.DMA
    tile = (8, LANES)
    results = pl.pallas_call(
        functools.partial(kernel, n, groups),
        out_shape=(
            jax.ShapeDtypeStruct(gradient.shape, half),
            jax.ShapeDtypeStruct(first_moment.shape, half),
            jax.ShapeDtypeStruct(second_moment.shape, half),
        ),
        in_specs=[anywhere] * 4 + [scalar] * 2,
        out_specs=(anywhere,) * 3,
        scratch_shapes=[
            pltpu.VMEM((share, cols), half),
            pltpu.VMEM((width, all_rows), half),
            pltpu.VMEM((width, all_rows), half),
            pltpu.VMEM((n, per_owner, SLAB, LANES), half),
            pltpu.VMEM((n * per_owner, SLAB, LANES), half),
            pltpu.VMEM((all_rows // span, span, BLOCK), half),
            pltpu.VMEM((halves, BLOCK // span, span, BLOCK), half),
            pltpu.VMEM((halves, all_rows, BLOCK), half),
            pltpu.VMEM((width, all_rows), half),
            pltpu.VMEM((width, all_rows), half),
            pltpu.VMEM((halves, all_rows, BLOCK), half),
            pltpu.VMEM(tile, jnp.float32),
            pltpu.VMEM((groups,) + tile, jnp.float32),
            pltpu.VMEM(tile, jnp.float32),
            pltpu.VMEM((n,) + tile, jnp.float32),
            dma((4 + 3 * halves,)),
            dma((n,)), dma((n,)),
            dma((n,)), dma((n,)),
            dma((halves, n)), dma((halves, n)),
            dma((halves, n)), dma((halves, n)),
            dma((halves, n)), dma((halves, n)),
            dma((groups,)), dma((groups,)),
            dma((n,)), dma((n,)),
        ],
        compiler_params=pltpu.CompilerParams(
            collective_id=0, has_side_effects=True, vmem_limit_bytes=32 << 20
        ),
    )(*[hbm(x) for x in (gradient, first_moment, second_moment, basis)], step_number, matrix_ids)
    return place(results)


def solution(mesh):
    in_specs = (
        P("group", "fsdp", None),
        P("group", "fsdp", None),
        P("group", "fsdp", None),
        P("group", "fsdp", None),
        P(),
        P("group"),
    )
    out_specs = (P("group", "fsdp", None), P("group", "fsdp", None), P("group", "fsdp", None))
    return jax.shard_map(local, mesh=mesh, in_specs=in_specs, out_specs=out_specs, check_vma=False)
```
